256 devices in a mesh: blk: 16 (over z_lo, x), rep: 16 (over y, z_hi, core).
Axes of the slice: x: 4, y: 4, z: 8 (z_hi: 2, z_lo: 4; z = z_hi * 4 + z_lo), core: 2. Of those that a mesh axis runs over, the one named last changes fastest.
Arguments:
- pixel_factors: float32 [196608, 256], P(('blk', 'rep')), may hold values from -1.5 to 1.5
- scene_factors: float32 [16384, 256], P('blk'), may hold values from -1.5 to 1.5
- elevations: bfloat16 [3, 196608, 1024], P(None, ('blk', 'rep')), may hold values from -6 to 6
- quality: bfloat16 [3, 196608, 1024], P(None, ('blk', 'rep')), may hold values from 0 to 1, as said below
- occupancy: int32 [3, 256], P(None, ('blk', 'rep')), may hold values from 0 to 1, as said below
Outputs:
- pixel_out: float32 [196608, 256], P(('blk', 'rep'))
- scene_out: float32 [16384, 256], P('blk')
The draws below stay inside these ranges and needn't reach their ends.
Inputs may be any that keep to these rules, and one draw needn't show every extreme that they name: quality is zero on every entry of an owner's tile whose occupancy is 0; otherwise about half of the entries are nonzero. occupancy is 0 or 1 and about three quarters of the tiles are occupied.
All inputs are finite; a program needn't handle non-finite values.
Results may differ from the reference program's by a relative error of at most 0.0003.
Values sent between devices are 32-bit elements; how exact they have to be, the bound alone decides.
No kernel may reach another device: no remote copies, remote signals or barrier semaphores. Data moves between devices by JAX's collectives and lax.ppermute only.
A program may use at most 64 MiB of HBM per device.

```python
import jax
import jax.numpy as jnp
from jax import lax

PIX_DEV = 768
ACQ_BLK = 1024
R = 256
STEPS = 3
PIX = 196608
ACQ = 16384
OWNERS = 256
GROUP_ROWS = 12288
N_BLK = 16


def occupied_tiles(key):
    tile_key = jax.random.fold_in(key, 11)
    return (jax.random.randint(tile_key, (STEPS, OWNERS), 0, 4) < 3).astype(jnp.int32)


def draw_occupancy(key, part):
    return occupied_tiles(key)


def draw_quality(key, part):
    owner_flags = occupied_tiles(key)
    seen = (jax.random.randint(jax.random.fold_in(key, 23), (STEPS, PIX, ACQ_BLK), 0, 20) < 11).astype(jnp.float32)
    mag_key = jax.random.fold_in(key, 37)
    magnitude = jax.random.uniform(mag_key, (STEPS, PIX, ACQ_BLK), jnp.float32, 0.2, 1.0)
    owner_rows = jnp.repeat(owner_flags.astype(jnp.float32), PIX_DEV, axis=1)
    return (magnitude * seen * owner_rows[:, :, None]).astype(jnp.bfloat16)


def block_levels(stream_key, shape, cuts, least, largest):
    gain, own = 1.0, jax.random.fold_in(stream_key, 6)
    for dim, parts in cuts:
        steps = jnp.exp(jax.random.uniform(jax.random.fold_in(own, dim), (parts,), jnp.float32, least / len(cuts), largest / len(cuts)))
        gain = gain * jnp.repeat(steps, shape[dim] // parts).reshape([-1 if axis == dim else 1 for axis in range(len(shape))])
    return gain


def noise(stream_key, dims, deviation, reach, shards=(), held_as=jnp.bfloat16):
    loudness = block_levels(stream_key, dims, shards, -0.22, 0.18) if shards else 1.0
    drawn = jax.random.normal(stream_key, dims, jnp.float32) * deviation * loudness
    return jnp.minimum(jnp.maximum(drawn, -reach), reach).astype(held_as)


def setup_inputs(seed: int = 0) -> dict:
    seeds = jax.random.split(jax.random.key(seed), 6)
    return {
        "pixel_factors": noise(seeds[0], (PIX, R), 0.25, 1.5, ((0, 256),), jnp.float32),
        "scene_factors": noise(seeds[1], (ACQ, R), 0.25, 1.5, ((0, 16),), jnp.float32),
        "elevations": noise(seeds[2], (STEPS, PIX, ACQ_BLK), 1.0, 6.0, ((1, 256),)),
        "quality": draw_quality(jax.random.fold_in(seeds[5], 71), 0),
        "occupancy": draw_occupancy(jax.random.fold_in(seeds[5], 71), 0),
    }


def group_update(args):
    pixel_rows, scene_block, tile_values, tile_quality, owner_flag = args
    weight = tile_quality.astype(jnp.float32) * owner_flag[:, None]
    predicted = jnp.dot(pixel_rows, scene_block.T, precision=lax.Precision.HIGHEST, preferred_element_type=jnp.float32)
    misfit = weight * (tile_values.astype(jnp.float32) - predicted)
    pixel_grad = jnp.dot(misfit, scene_block, precision=lax.Precision.HIGHEST, preferred_element_type=jnp.float32)
    scene_grad = jnp.dot(misfit.T, pixel_rows, precision=lax.Precision.HIGHEST, preferred_element_type=jnp.float32)
    new_pixels = pixel_rows + (8.0 / ACQ_BLK) * pixel_grad
    new_scene = scene_block + (8.0 / GROUP_ROWS) * scene_grad
    return new_pixels, new_scene


def reference(pixel_factors, scene_factors, elevations, quality, occupancy):
    pixels = pixel_factors.reshape(N_BLK, GROUP_ROWS, R)
    scenes = scene_factors.reshape(N_BLK, ACQ_BLK, R)
    owner_rows = jnp.repeat(occupancy.astype(jnp.float32), PIX_DEV, axis=1).reshape(STEPS, N_BLK, GROUP_ROWS)
    tiles = elevations.reshape(STEPS, N_BLK, GROUP_ROWS, ACQ_BLK)
    weights = quality.reshape(STEPS, N_BLK, GROUP_ROWS, ACQ_BLK)
    for step_index in range(STEPS):
        paired = jnp.roll(scenes, -step_index, axis=0)
        pixels, paired = lax.map(group_update, (pixels, paired, tiles[step_index], weights[step_index], owner_rows[step_index]))
        scenes = jnp.roll(paired, step_index, axis=0)
    return pixels.reshape(PIX, R), scenes.reshape(ACQ, R)
```

```python
import functools

import jax
import jax.numpy as jnp
from jax import lax
from jax.experimental import pallas as pl
from jax.experimental.pallas import tpu as pltpu
from jax.sharding import PartitionSpec as P

PIX_DEV = 768
ACQ_BLK = 1024
R = 256
STEPS = 3
GROUP_ROWS = 12288
N_BLK = 16
N_Y = 4
N_ZH = 2
N_CORE = 2
N_REP = N_Y * N_ZH * N_CORE
CHUNK = 128
PAIR = 2 * CHUNK
ROW_TILE = 256
BOTH = ("blk", "rep")
ORDER = (2, 1, 3)


VMEM = pl.BlockSpec(memory_space=pltpu.VMEM)
SMEM = pl.BlockSpec(memory_space=pltpu.SMEM)
HBM = pl.BlockSpec(memory_space=pltpu.HBM)
ANY = pl.BlockSpec(memory_space=pl.ANY)

F32, BF16 = jnp.float32, jnp.bfloat16
PIXELS = jax.ShapeDtypeStruct((PIX_DEV, R), F32)
HALF = jax.ShapeDtypeStruct((PIX_DEV, R), BF16)
TURNED = jax.ShapeDtypeStruct((R, PIX_DEV), BF16)
TILES = jax.ShapeDtypeStruct((N_Y, PIX_DEV, PAIR), BF16)
BLOCK = jax.ShapeDtypeStruct((R, PAIR), BF16)
MISFIT = jax.ShapeDtypeStruct((PIX_DEV, PAIR), BF16)
PIECE = jax.ShapeDtypeStruct((R, CHUNK), F32)
ROWS = jax.ShapeDtypeStruct((CHUNK, R), F32)
TOKEN = jax.ShapeDtypeStruct((8, 128), F32)
FLOPS = 3 * 2 * PIX_DEV * ACQ_BLK * R


def moved(value, blk=0, y=0, zh=0, core=0):
    pairs = []
    for b in range(N_BLK):
        for r in range(N_REP):
            ry, rz, rc = r // (N_ZH * N_CORE), (r // N_CORE) % N_ZH, r % N_CORE
            db = (b + blk) % N_BLK
            dr = (((ry + y) % N_Y) * N_ZH + (rz + zh) % N_ZH) * N_CORE + (rc + core) % N_CORE
            pairs.append((b * N_REP + r, db * N_REP + dr))
    return lax.ppermute(value, BOTH, pairs)


def position():
    rep = lax.axis_index("rep")
    return lax.rem(rep, N_CORE), lax.div(rep, N_ZH * N_CORE)


def split(value):
    high = value.astype(BF16)
    low = (value - high.astype(F32)).astype(BF16)
    return high, low


NN = (((1,), (0,)), ((), ()))
NT = (((1,), (1,)), ((), ()))


def dot3(a_high, a_low, b_high, b_low, dims):
    dot = functools.partial(lax.dot_general, dimension_numbers=dims, preferred_element_type=F32)
    return dot(a_high, b_high) + (dot(a_high, b_low) + dot(a_low, b_high))


def call(kernel, out, in_specs, out_specs, name, args, mib=4, flops=0, scratch=()):
    return pl.pallas_call(
        kernel,
        out_shape=out,
        in_specs=in_specs,
        out_specs=out_specs,
        scratch_shapes=list(scratch),
        compiler_params=pltpu.CompilerParams(vmem_limit_bytes=mib << 20),
        cost_estimate=pl.CostEstimate(flops=flops, bytes_accessed=1 << 20, transcendentals=0),
        name=name,
    )(*args)


def prepare_kernel(pixels, scene, uh, ul, uth, utl, vh, vl, own):
    core, y = position()
    for r in range(N_Y):
        at = lax.rem(y + r, N_Y) * PAIR
        vh[r], vl[r] = split(scene[pl.ds(pl.multiple_of(at, PAIR), PAIR), :].T)
    own[...] = scene[pl.ds(pl.multiple_of(y * PAIR + core * CHUNK, CHUNK), CHUNK), :].T
    for t in range(PIX_DEV // ROW_TILE):
        rows = pl.ds(t * ROW_TILE, ROW_TILE)
        value = pixels[rows, :]
        uh[rows, :], ul[rows, :] = split(value)
        uth[:, rows], utl[:, rows] = split(value.T)


def prepare(pixels, scene):
    blocks = jax.ShapeDtypeStruct((N_Y, R, PAIR), BF16)
    out = [HALF, HALF, TURNED, TURNED, blocks, blocks, PIECE]
    res = call(prepare_kernel, out, [VMEM] * 2, [VMEM] * len(out), "prepare", (pixels, scene))
    return res[:4], res[4:6], res[6]


def misfit_body(step, r, occupancy, factors, v_high, v_low, tile, weight, sent, kept, mh, ml, grad):
    core, y = position()
    uh, ul, uth, utl = factors
    flag = occupancy[step, 0].astype(F32)
    columns = pl.ds(pl.multiple_of(lax.rem(y + r, N_Y) * PAIR, PAIR), PAIR)
    grad[...] = jnp.zeros_like(grad)

    @pl.loop(0, PIX_DEV // ROW_TILE)
    def _(t):
        rows = pl.ds(pl.multiple_of(t * ROW_TILE, ROW_TILE), ROW_TILE)
        predicted = dot3(uh[rows, :], ul[rows, :], v_high[...], v_low[...], NN)
        misfit = (weight[rows, columns].astype(F32) * flag) * (tile[rows, columns].astype(F32) - predicted)
        m_high, m_low = split(misfit)
        mh[rows, :] = m_high
        ml[rows, :] = m_low
        grad[...] += dot3(uth[:, rows], utl[:, rows], m_high, m_low, NN)

    left, right = grad[:, :CHUNK], grad[:, CHUNK:]
    kept[...] = jnp.where(core == 0, left, right)
    sent[...] = jnp.where(core == 0, right, left)


def misfit_first_kernel(step, r, occupancy, uh, ul, uth, utl, vh, vl, tile, weight, after, *outs):
    misfit_body(step, r, occupancy, (uh, ul, uth, utl), vh.at[r], vl.at[r], tile, weight, *outs)


def misfit_kernel(step, r, occupancy, uh, ul, uth, utl, mine, other, tile, weight, after, *outs):
    core, _ = position()
    sent, kept, mh, ml, vh, vl, grad = outs
    first = jnp.where(core == 0, mine[...], other[...])
    second = jnp.where(core == 0, other[...], mine[...])
    vh[...], vl[...] = split(jnp.concatenate([first, second], axis=1))
    misfit_body(step, r, occupancy, (uh, ul, uth, utl), vh, vl, tile, weight, sent, kept, mh, ml, grad)


def misfit_part(step, r, occupancy, factors, block, tiles, after):
    kernel = misfit_kernel if step else misfit_first_kernel
    out = [PIECE, PIECE, MISFIT, MISFIT] + ([BLOCK, BLOCK] if step else [])
    return call(
        functools.partial(kernel, step, r),
        out,
        [SMEM] + [VMEM] * 8 + [ANY],
        [VMEM] * len(out),
        f"misfit{step}_{r}",
        (occupancy, *factors, *block, *tiles, after),
        flops=FLOPS // 2,
        scratch=[pltpu.VMEM((R, PAIR), F32)],
    )


def pixel_kernel(step, pixels, *refs):
    last = step + 1 == STEPS
    mh, ml = refs[:N_Y], refs[N_Y : 2 * N_Y]
    refs = refs[2 * N_Y :]
    if step:
        vh, vl = refs[:N_Y], refs[N_Y : 2 * N_Y]
        refs = refs[2 * N_Y :]
    else:
        vh, vl = [refs[0].at[k] for k in range(N_Y)], [refs[1].at[k] for k in range(N_Y)]
        refs = refs[2:]
    outs = refs[1:]
    outs[0][...] = jnp.zeros_like(outs[0])
    for t in range(PIX_DEV // ROW_TILE):
        rows = pl.ds(t * ROW_TILE, ROW_TILE)
        grad = jnp.zeros((ROW_TILE, R), F32)
        for k in range(N_Y):
            grad = grad + dot3(mh[k][rows, :], ml[k][rows, :], vh[k][...], vl[k][...], NT)
        value = pixels[rows, :] + (8.0 / ACQ_BLK) * grad
        outs[1][rows, :] = value
        if not last:
            outs[2][rows, :], outs[3][rows, :] = split(value)
            outs[4][:, rows], outs[5][:, rows] = split(value.T)


def pixel_step(step, pixels, mh, ml, blocks, after):
    last = step + 1 == STEPS
    ins = [pixels, *mh, *ml, *blocks, after]
    out = [TOKEN, PIXELS]
    if not last:
        out += [HALF, HALF, TURNED, TURNED]
    res = call(
        functools.partial(pixel_kernel, step),
        out,
        [VMEM] * (len(ins) - 1) + [ANY],
        [VMEM] * len(out),
        f"pixels{step}",
        ins,
        flops=FLOPS,
    )
    return res[0], res[1], res[2:]


def add_kernel(a, b, out):
    out[...] = a[...] + b[...]


def total_kernel(own, kept, other, first, second, third, out):
    total = (kept[...] + other[...]) + (first[...] + (second[...] + third[...]))
    out[...] = 0.5 * own[...] + (8.0 / GROUP_ROWS) * total


def fresh_kernel(last, a, b, after, out):
    value = a[...] + b[...]
    out[...] = value.T if last else value


def assemble_kernel(*refs):
    core, y = position()
    pieces, out, sems = refs[: 2 * N_Y], refs[2 * N_Y], refs[2 * N_Y + 1]
    copies = []
    for r in range(N_Y):
        for k in range(N_CORE):
            at = lax.rem(y + r, N_Y) * PAIR + lax.rem(core + k, N_CORE) * CHUNK
            rows = pl.ds(pl.multiple_of(at, CHUNK), CHUNK)
            copies.append(pltpu.make_async_copy(pieces[k * N_Y + r], out.at[rows, :], sems.at[k, r]))
    for c in copies:
        c.start()
    for c in copies:
        c.wait()


def per_device(pixel_factors, scene_factors, elevations, quality, occupancy):
    pixels = pixel_factors
    factors, blocks, own = prepare(pixel_factors, scene_factors)
    mine = other = None
    for step in range(STEPS):
        last = step + 1 == STEPS
        tiles = elevations[step], quality[step]
        parts, sums = {}, {}
        order = (0,) + ORDER if step else ORDER + (0,)
        swapped = {}
        for n, r in enumerate(order):
            after = own
            if n > 1 and order[n - 2]:
                p = order[n - 2]
                after = sums[p] = call(
                    add_kernel, PIECE, [VMEM] * 2, VMEM, f"add{step}_{p}", (parts[p][1], swapped[p])
                )
            block = (mine[r], other[r]) if step else blocks
            parts[r] = misfit_part(step, r, occupancy, factors, block, tiles, after)
            swapped[r] = moved(parts[r][0], core=1)
        if step:
            blocks = [parts[r][4] for r in range(N_Y)] + [parts[r][5] for r in range(N_Y)]
        arrived = []
        for r in ORDER:
            if r not in sums:
                sums[r] = call(add_kernel, PIECE, [VMEM] * 2, VMEM, f"add{step}_{r}", (parts[r][1], swapped[r]))
            arrived.append(moved(sums[r], y=r))
        half = call(
            total_kernel, PIECE, [VMEM] * 6, VMEM, f"total{step}", (own, parts[0][1], swapped[0], *arrived)
        )
        go = STEPS - 1 if last else -1
        near, far = moved(half, blk=go, zh=1), moved(half, blk=go)
        token, pixels, factors = pixel_step(
            step,
            pixels,
            [parts[r][2] for r in range(N_Y)],
            [parts[r][3] for r in range(N_Y)],
            blocks,
            half,
        )
        own = call(
            functools.partial(fresh_kernel, last),
            ROWS if last else PIECE,
            [VMEM] * 2 + [ANY],
            VMEM,
            f"fresh{step}",
            (near, far, token),
        )
        mine = {0: own}
        for r in ORDER:
            mine[r] = moved(own, y=-r)
        other = {r: moved(mine[r], core=1) for r in (0,) + ORDER}
    scene = call(
        assemble_kernel,
        jax.ShapeDtypeStruct((ACQ_BLK, R), F32),
        [VMEM] * (2 * N_Y),
        HBM,
        "assemble",
        [mine[r] for r in range(N_Y)] + [other[r] for r in range(N_Y)],
        scratch=[pltpu.SemaphoreType.DMA((N_CORE, N_Y))],
    )
    return (pixels, scene)


def solution(mesh):
    in_specs = (
        P(("blk", "rep"), None),
        P("blk", None),
        P(None, ("blk", "rep"), None),
        P(None, ("blk", "rep"), None),
        P(None, ("blk", "rep")),
    )
    out_specs = (P(("blk", "rep"), None), P("blk", None))
    return jax.shard_map(
        per_device, mesh=mesh, in_specs=in_specs, out_specs=out_specs, check_vma=False
    )
```

```python
import functools

import jax
import jax.numpy as jnp
from jax import lax
from jax.experimental import pallas as pl
from jax.experimental.pallas import tpu as pltpu
from jax.sharding import PartitionSpec as P


PIX_DEV = 768
ACQ_BLK = 1024
R = 256
STEPS = 3
GROUP_ROWS = 12288
N_BLK = 16
N_Y = 4
N_ZH = 2
N_CORE = 2
N_REP = N_Y * N_ZH * N_CORE
CHUNK = 128
PAIR = 2 * CHUNK
ROW_TILE = 256
BOTH = ("blk", "rep")
ORDER = (2, 1, 3)
CALLS = (((2, 1), (3, 0)), ((0,), (2, 1), (3,)), ((0,), (2, 1), (3,)))


VMEM = pl.BlockSpec(memory_space=pltpu.VMEM)
SMEM = pl.BlockSpec(memory_space=pltpu.SMEM)
HBM = pl.BlockSpec(memory_space=pltpu.HBM)
ANY = pl.BlockSpec(memory_space=pl.ANY)

F32, BF16 = jnp.float32, jnp.bfloat16
PIXELS = jax.ShapeDtypeStruct((PIX_DEV, R), F32)
HALF = jax.ShapeDtypeStruct((PIX_DEV, R), BF16)
TURNED = jax.ShapeDtypeStruct((R, PIX_DEV), BF16)
PIECE = jax.ShapeDtypeStruct((R, CHUNK), F32)
ROWS = jax.ShapeDtypeStruct((CHUNK, R), F32)
TOKEN = jax.ShapeDtypeStruct((8, 128), F32)
FLOPS = 3 * 2 * PIX_DEV * ACQ_BLK * R


def moved(value, blk=0, y=0, zh=0, core=0):
    pairs = []
    for b in range(N_BLK):
        for r in range(N_REP):
            ry, rz, rc = r // (N_ZH * N_CORE), (r // N_CORE) % N_ZH, r % N_CORE
            db = (b + blk) % N_BLK
            dr = (((ry + y) % N_Y) * N_ZH + (rz + zh) % N_ZH) * N_CORE + (rc + core) % N_CORE
            pairs.append((b * N_REP + r, db * N_REP + dr))
    return lax.ppermute(value, BOTH, pairs)


def position():
    rep = lax.axis_index("rep")
    return lax.rem(rep, N_CORE), lax.div(rep, N_ZH * N_CORE)


def split(value):
    high = value.astype(BF16)
    low = (value - high.astype(F32)).astype(BF16)
    return high, low


NN = (((1,), (0,)), ((), ()))
NT = (((1,), (1,)), ((), ()))


def dot3(a_high, a_low, b_high, b_low, dims):
    dot = functools.partial(lax.dot_general, dimension_numbers=dims, preferred_element_type=F32)
    return dot(a_high, b_high) + (dot(a_high, b_low) + dot(a_low, b_high))


def call(kernel, out, in_specs, out_specs, args, mib=4, flops=0, scratch=()):
    return pl.pallas_call(
        kernel,
        out_shape=out,
        in_specs=in_specs,
        out_specs=out_specs,
        scratch_shapes=list(scratch),
        compiler_params=pltpu.CompilerParams(vmem_limit_bytes=mib << 20),
        cost_estimate=pl.CostEstimate(flops=flops, bytes_accessed=1 << 20, transcendentals=0),
    )(*args)


def prepare_kernel(pixels, scene, uh, ul, uth, utl, vh, vl, own):
    core, y = position()
    for r in range(N_Y):
        at = lax.rem(y + r, N_Y) * PAIR
        vh[r], vl[r] = split(scene[pl.ds(pl.multiple_of(at, PAIR), PAIR), :].T)
    own[...] = scene[pl.ds(pl.multiple_of(y * PAIR + core * CHUNK, CHUNK), CHUNK), :].T
    for t in range(PIX_DEV // ROW_TILE):
        rows = pl.ds(t * ROW_TILE, ROW_TILE)
        value = pixels[rows, :]
        uh[rows, :], ul[rows, :] = split(value)
        uth[:, rows], utl[:, rows] = split(value.T)


def prepare(pixels, scene):
    blocks = jax.ShapeDtypeStruct((N_Y, R, PAIR), BF16)
    out = [HALF, HALF, TURNED, TURNED, blocks, blocks, PIECE]
    res = call(prepare_kernel, out, [VMEM] * 2, [VMEM] * len(out), (pixels, scene))
    return res[:4], res[4:6], res[6]


def misfit_kernel(step, chunks, carried, occupancy, uh, ul, uth, utl, tile, weight, *refs):
    core, y = position()
    count = len(chunks)
    if step:
        mine, other, refs = refs[:count], refs[count : 2 * count], refs[2 * count :]
        refs, (vh, vl) = refs[:-2], refs[-2:]
        for k in range(count):
            first = jnp.where(core == 0, mine[k][...], other[k][...])
            second = jnp.where(core == 0, other[k][...], mine[k][...])
            vh[k], vl[k] = split(jnp.concatenate([first, second], axis=1))
    else:
        (vh, vl), refs = refs[:2], refs[2:]
    sent, kept, mh, ml = refs[-4:]
    if carried:
        sent[count] = refs[0][0]
    flag = occupancy[step, 0].astype(F32)

    def one(k, r, at):
        columns = pl.ds(pl.multiple_of(lax.rem(y + r, N_Y) * PAIR, PAIR), PAIR)
        v_high, v_low = vh[at], vl[at]
        predicted = dot3(uh[...], ul[...], v_high, v_low, NN)
        misfit = (weight[:, columns].astype(F32) * flag) * (tile[:, columns].astype(F32) - predicted)
        m_high, m_low = split(misfit)
        mh[k] = m_high
        ml[k] = m_low
        grad = dot3(uth[...], utl[...], m_high, m_low, NN)
        left, right = grad[:, :CHUNK], grad[:, CHUNK:]
        kept[k] = jnp.where(core == 0, left, right)
        sent[k] = jnp.where(core == 0, right, left)

    if count == 1:
        one(0, chunks[0], 0 if step else chunks[0])
    else:

        @pl.loop(0, count)
        def _(k):
            r = chunks[0] + k * (chunks[1] - chunks[0])
            one(k, r, k if step else r)


def misfit_part(step, chunks, occupancy, factors, tiles, block, carried, before):
    count = len(chunks)
    pieces = lambda n: jax.ShapeDtypeStruct((n, R, CHUNK), F32)
    misfits = jax.ShapeDtypeStruct((count, PIX_DEV, PAIR), BF16)
    blocks = jax.ShapeDtypeStruct((count, R, PAIR), BF16)
    out = [pieces(count + len(carried)), pieces(count), misfits, misfits] + ([blocks] * 2 if step else [])
    ins = [occupancy, *factors, *tiles, *block, *carried]
    return call(
        functools.partial(misfit_kernel, step, chunks, len(carried)),
        out,
        [SMEM] + [VMEM] * (len(ins) - 1) + [ANY] * len(before),
        [VMEM] * len(out),
        (*ins, *before),
        mib=6,
        flops=FLOPS * count // 2,
    )


def pixel_kernel(step, pixels, *refs):
    last = step + 1 == STEPS
    calls = len(CALLS[step])
    rows_of = [(n, k) for n, chunks in enumerate(CALLS[step]) for k in range(len(chunks))]
    mh, ml, refs = refs[:calls], refs[calls : 2 * calls], refs[2 * calls :]
    if step:
        vh, vl, refs = refs[:calls], refs[calls : 2 * calls], refs[2 * calls :]
    else:
        vh, vl, refs = refs[0], refs[1], refs[2:]
    outs = refs[1:]
    outs[0][...] = jnp.zeros_like(outs[0])

    @pl.loop(0, PIX_DEV // ROW_TILE)
    def _(t):
        rows = pl.ds(pl.multiple_of(t * ROW_TILE, ROW_TILE), ROW_TILE)
        grad = jnp.zeros((ROW_TILE, R), F32)
        for n, k in rows_of:
            r = CALLS[step][n][k]
            v_high, v_low = (vh[n][k], vl[n][k]) if step else (vh[r], vl[r])
            grad = grad + dot3(mh[n][k, rows, :], ml[n][k, rows, :], v_high, v_low, NT)
        value = pixels[rows, :] + (8.0 / ACQ_BLK) * grad
        outs[1][rows, :] = value
        if not last:
            outs[2][rows, :], outs[3][rows, :] = split(value)
            outs[4][:, rows], outs[5][:, rows] = split(value.T)


def pixel_step(step, pixels, parts, blocks, after):
    last = step + 1 == STEPS
    ins = [pixels, *(p[2] for p in parts), *(p[3] for p in parts), *blocks, after]
    out = [TOKEN, PIXELS]
    if not last:
        out += [HALF, HALF, TURNED, TURNED]
    res = call(
        functools.partial(pixel_kernel, step),
        out,
        [VMEM] * (len(ins) - 1) + [ANY],
        [VMEM] * len(out),
        ins,
        flops=FLOPS,
    )
    return res[0], res[1], res[2:]


def add_kernel(*refs):
    kept, swapped, first, second = refs[:-3], *refs[-3:]
    first[...] = kept[0][0] + swapped[0]
    second[...] = kept[-1][-1 % kept[-1].shape[0]] + swapped[1]


def add_pair(kept, swapped):
    return call(add_kernel, [PIECE] * 2, [VMEM] * (len(kept) + 1), [VMEM] * 2, (*kept, swapped))


def total_kernel(own, summed, first, second, third, out):
    total = summed[...] + (first[...] + (second[...] + third[...]))
    out[...] = 0.5 * own[...] + (8.0 / GROUP_ROWS) * total


def fresh_kernel(last, a, b, after, out):
    value = a[...] + b[...]
    out[...] = value.T if last else value


def join_kernel(*refs):
    for r in range(N_Y):
        refs[-1][r] = refs[r][...]


def assemble_kernel(mine, other, out, sems):
    core, y = position()
    copies = []
    for r in range(N_Y):
        for k, pieces in enumerate((mine, other)):
            at = lax.rem(y + r, N_Y) * PAIR + lax.rem(core + k, N_CORE) * CHUNK
            rows = pl.ds(pl.multiple_of(at, CHUNK), CHUNK)
            copies.append(pltpu.make_async_copy(pieces.at[r], out.at[rows, :], sems.at[k, r]))
    for c in copies:
        c.start()
    for c in copies:
        c.wait()


def steps(pixel_factors, scene_factors, elevations, quality, occupancy):
    pixels = pixel_factors
    factors, blocks, own = prepare(pixel_factors, scene_factors)
    tiles = elevations[0], quality[0]
    mine = other = None
    for step in range(STEPS):
        last = step + 1 == STEPS
        parts = []
        for n, chunks in enumerate(CALLS[step]):
            block = [mine[r] for r in chunks] + [other[r] for r in chunks] if step else blocks
            carried = [parts[0][0]] if step and n == 2 else []
            before = [parts[-1][1]] if parts else []
            parts.append(misfit_part(step, chunks, occupancy, factors, tiles, block, carried, before))
        if step:
            blocks = [p[4] for p in parts] + [p[5] for p in parts]
        kept = [p[1] for p in parts]
        early = moved(parts[-2][0], core=1)
        late = moved(parts[-1][0], core=1)
        sums = add_pair(kept[-2:-1], early)
        arrived = [moved(v, y=r) for r, v in zip(ORDER, sums)]
        sums = add_pair([kept[-1], kept[0]] if step else kept[-1:], late)
        arrived.append(moved(sums[0], y=ORDER[2]))
        half = call(total_kernel, PIECE, [VMEM] * 5, VMEM, (own, sums[1], *arrived))
        go = STEPS - 1 if last else -1
        far, near = moved(half, blk=go, zh=1), moved(half, blk=go)
        token, pixels, factors = pixel_step(step, pixels, parts, blocks, half)
        if not last:
            elevations, quality, token = lax.optimization_barrier((elevations, quality, token))
            tiles = elevations[step + 1], quality[step + 1]
        own = call(
            functools.partial(fresh_kernel, last),
            ROWS if last else PIECE,
            [VMEM] * 2 + [ANY],
            VMEM,
            (near, far, token),
        )
        mine, other = {0: own}, {}
        if not last:
            other[0] = moved(own, core=1)
        for r in ORDER:
            mine[r] = moved(own, y=-r)
        if not last:
            for r in ORDER:
                other[r] = moved(mine[r], core=1)
    joined = jax.ShapeDtypeStruct((N_Y, CHUNK, R), F32)
    joined = call(join_kernel, joined, [VMEM] * N_Y, VMEM, [mine[r] for r in range(N_Y)])
    scene = call(
        assemble_kernel,
        jax.ShapeDtypeStruct((ACQ_BLK, R), F32),
        [VMEM] * 2,
        HBM,
        (joined, moved(joined, core=1)),
        scratch=[pltpu.SemaphoreType.DMA((N_CORE, N_Y))],
    )
    return (pixels, scene)


def solution(mesh):
    in_specs = (
        P(("blk", "rep"), None),
        P("blk", None),
        P(None, ("blk", "rep"), None),
        P(None, ("blk", "rep"), None),
        P(None, ("blk", "rep")),
    )
    out_specs = (P(("blk", "rep"), None), P("blk", None))
    return jax.shard_map(steps, mesh=mesh, in_specs=in_specs, out_specs=out_specs, check_vma=False)
```

```python
import functools

import jax
import jax.numpy as jnp
from jax import lax
from jax.experimental import pallas as pl
from jax.experimental.pallas import tpu as pltpu
from jax.sharding import PartitionSpec as P


PIX_DEV = 768
ACQ_BLK = 1024
R = 256
STEPS = 3
GROUP_ROWS = 12288
N_BLK = 16
N_Y = 4
N_ZH = 2
N_CORE = 2
N_REP = N_Y * N_ZH * N_CORE
CHUNK = 128
PAIR = 2 * CHUNK
ROW_TILE = 256
BOTH = ("blk", "rep")
ORDER = (2, 1, 3)
CALLS = (((2,), (0,), (1, 3)), ((0,), (2,), (1, 3)), ((0,), (2,), (1, 3)))


VMEM = pl.BlockSpec(memory_space=pltpu.VMEM)
SMEM = pl.BlockSpec(memory_space=pltpu.SMEM)
HBM = pl.BlockSpec(memory_space=pltpu.HBM)
ANY = pl.BlockSpec(memory_space=pl.ANY)

F32, BF16 = jnp.float32, jnp.bfloat16
PIXELS = jax.ShapeDtypeStruct((PIX_DEV, R), F32)
HALF = jax.ShapeDtypeStruct((PIX_DEV, R), BF16)
TURNED = jax.ShapeDtypeStruct((R, PIX_DEV), BF16)
PIECE = jax.ShapeDtypeStruct((R, CHUNK), F32)
ROWS = jax.ShapeDtypeStruct((CHUNK, R), F32)
TOKEN = jax.ShapeDtypeStruct((8, 128), F32)
FLOPS = 3 * 2 * PIX_DEV * ACQ_BLK * R


def moved(value, blk=0, y=0, zh=0, core=0):
    pairs = []
    for b in range(N_BLK):
        for r in range(N_REP):
            ry, rz, rc = r // (N_ZH * N_CORE), (r // N_CORE) % N_ZH, r % N_CORE
            db = (b + blk) % N_BLK
            dr = (((ry + y) % N_Y) * N_ZH + (rz + zh) % N_ZH) * N_CORE + (rc + core) % N_CORE
            pairs.append((b * N_REP + r, db * N_REP + dr))
    return lax.ppermute(value, BOTH, pairs)


def position():
    rep = lax.axis_index("rep")
    return lax.rem(rep, N_CORE), lax.div(rep, N_ZH * N_CORE)


def split(value):
    high = value.astype(BF16)
    low = (value - high.astype(F32)).astype(BF16)
    return high, low


NN = (((1,), (0,)), ((), ()))
NT = (((1,), (1,)), ((), ()))


def dot3(a_high, a_low, b_high, b_low, dims):
    dot = functools.partial(lax.dot_general, dimension_numbers=dims, preferred_element_type=F32)
    return dot(a_high, b_high) + (dot(a_high, b_low) + dot(a_low, b_high))


def call(kernel, out, in_specs, out_specs, args, mib=4, flops=0, scratch=()):
    return pl.pallas_call(
        kernel,
        out_shape=out,
        in_specs=in_specs,
        out_specs=out_specs,
        scratch_shapes=list(scratch),
        compiler_params=pltpu.CompilerParams(vmem_limit_bytes=mib << 20),
        cost_estimate=pl.CostEstimate(flops=flops, bytes_accessed=1 << 20, transcendentals=0),
    )(*args)


def prepare_kernel(pixels, scene, before, uh, ul, uth, utl, vh, vl, own):
    core, y = position()
    for r in range(N_Y):
        at = lax.rem(y + r, N_Y) * PAIR
        vh[r], vl[r] = split(scene[pl.ds(pl.multiple_of(at, PAIR), PAIR), :].T)
    own[...] = scene[pl.ds(pl.multiple_of(y * PAIR + core * CHUNK, CHUNK), CHUNK), :].T
    for t in range(PIX_DEV // ROW_TILE):
        rows = pl.ds(t * ROW_TILE, ROW_TILE)
        value = pixels[rows, :]
        uh[rows, :], ul[rows, :] = split(value)
        uth[:, rows], utl[:, rows] = split(value.T)


def prepare(pixels, scene, before):
    blocks = jax.ShapeDtypeStruct((N_Y, R, PAIR), BF16)
    out = [HALF, HALF, TURNED, TURNED, blocks, blocks, PIECE]
    res = call(prepare_kernel, out, [VMEM] * 2 + [ANY], [VMEM] * len(out), (pixels, scene, before))
    return res[:4], res[4:6], res[6]


def misfit_kernel(step, chunks, carried, occupancy, uh, ul, uth, utl, tile, weight, *refs):
    core, y = position()
    count = len(chunks)
    if step:
        mine, other, refs = refs[:count], refs[count : 2 * count], refs[2 * count :]
        refs, (vh, vl) = refs[:-2], refs[-2:]
        for k in range(count):
            first = jnp.where(core == 0, mine[k][...], other[k][...])
            second = jnp.where(core == 0, other[k][...], mine[k][...])
            vh[k], vl[k] = split(jnp.concatenate([first, second], axis=1))
    else:
        (vh, vl), refs = refs[:2], refs[2:]
    sent, kept, mh, ml = refs[-4:]
    if carried:
        sent[count] = refs[0][0]
    flag = occupancy[step, 0].astype(F32)

    def one(k, r, at):
        columns = pl.ds(pl.multiple_of(lax.rem(y + r, N_Y) * PAIR, PAIR), PAIR)
        v_high, v_low = vh[at], vl[at]
        predicted = dot3(uh[...], ul[...], v_high, v_low, NN)
        misfit = (weight[:, columns].astype(F32) * flag) * (tile[:, columns].astype(F32) - predicted)
        m_high, m_low = split(misfit)
        mh[k] = m_high
        ml[k] = m_low
        grad = dot3(uth[...], utl[...], m_high, m_low, NN)
        left, right = grad[:, :CHUNK], grad[:, CHUNK:]
        kept[k] = jnp.where(core == 0, left, right)
        sent[k] = jnp.where(core == 0, right, left)

    if count == 1:
        one(0, chunks[0], 0 if step else chunks[0])
    else:

        @pl.loop(0, count)
        def _(k):
            r = chunks[0] + k * (chunks[1] - chunks[0])
            one(k, r, k if step else r)


def misfit_part(step, chunks, occupancy, factors, tiles, block, carried, before):
    count = len(chunks)
    pieces = lambda n: jax.ShapeDtypeStruct((n, R, CHUNK), F32)
    misfits = jax.ShapeDtypeStruct((count, PIX_DEV, PAIR), BF16)
    blocks = jax.ShapeDtypeStruct((count, R, PAIR), BF16)
    out = [pieces(count + len(carried)), pieces(count), misfits, misfits] + ([blocks] * 2 if step else [])
    ins = [occupancy, *factors, *tiles, *block, *carried]
    return call(
        functools.partial(misfit_kernel, step, chunks, len(carried)),
        out,
        [SMEM] + [VMEM] * (len(ins) - 1) + [ANY] * len(before),
        [VMEM] * len(out),
        (*ins, *before),
        mib=6,
        flops=FLOPS * count // 2,
    )


def pixel_kernel(step, pixels, *refs):
    last = step + 1 == STEPS
    calls = len(CALLS[step])
    rows_of = [(n, k) for n, chunks in enumerate(CALLS[step]) for k in range(len(chunks))]
    mh, ml, refs = refs[:calls], refs[calls : 2 * calls], refs[2 * calls :]
    if step:
        vh, vl, refs = refs[:calls], refs[calls : 2 * calls], refs[2 * calls :]
    else:
        vh, vl, refs = refs[0], refs[1], refs[2:]
    outs = refs[1:]
    outs[0][...] = jnp.zeros_like(outs[0])

    @pl.loop(0, PIX_DEV // ROW_TILE)
    def _(t):
        rows = pl.ds(pl.multiple_of(t * ROW_TILE, ROW_TILE), ROW_TILE)
        grad = jnp.zeros((ROW_TILE, R), F32)
        for n, k in rows_of:
            r = CALLS[step][n][k]
            v_high, v_low = (vh[n][k], vl[n][k]) if step else (vh[r], vl[r])
            grad = grad + dot3(mh[n][k, rows, :], ml[n][k, rows, :], v_high, v_low, NT)
        value = pixels[rows, :] + (8.0 / ACQ_BLK) * grad
        outs[1][rows, :] = value
        if not last:
            outs[2][rows, :], outs[3][rows, :] = split(value)
            outs[4][:, rows], outs[5][:, rows] = split(value.T)


def pixel_step(step, pixels, parts, blocks, after):
    last = step + 1 == STEPS
    ins = [pixels, *(p[2] for p in parts), *(p[3] for p in parts), *blocks, after]
    out = [TOKEN, PIXELS]
    if not last:
        out += [HALF, HALF, TURNED, TURNED]
    res = call(
        functools.partial(pixel_kernel, step),
        out,
        [VMEM] * (len(ins) - 1) + [ANY],
        [VMEM] * len(out),
        ins,
        flops=FLOPS,
    )
    return res[0], res[1], res[2:]


def add_first_kernel(kept, swapped, out):
    out[...] = kept[0] + swapped[0]


def add_rest_kernel(kept, own, swapped, first, second, third):
    first[...] = kept[0] + swapped[0]
    second[...] = kept[1] + swapped[1]
    third[...] = own[0] + swapped[2]


def total_kernel(own, summed, first, second, third, out):
    total = summed[...] + (first[...] + (second[...] + third[...]))
    out[...] = 0.5 * own[...] + (8.0 / GROUP_ROWS) * total


def fresh_kernel(last, a, b, after, out):
    value = a[...] + b[...]
    out[...] = value.T if last else value


def join_kernel(*refs):
    for r in range(N_Y):
        refs[-1][r] = refs[r][...]


def assemble_kernel(mine, other, out, sems):
    core, y = position()
    copies = []
    for r in range(N_Y):
        for k, pieces in enumerate((mine, other)):
            at = lax.rem(y + r, N_Y) * PAIR + lax.rem(core + k, N_CORE) * CHUNK
            rows = pl.ds(pl.multiple_of(at, CHUNK), CHUNK)
            copies.append(pltpu.make_async_copy(pieces.at[r], out.at[rows, :], sems.at[k, r]))
    for c in copies:
        c.start()
    for c in copies:
        c.wait()


def steps(pixel_factors, scene_factors, elevations, quality, occupancy):
    pixels = pixel_factors
    tiles = elevations[0], quality[0]
    factors, blocks, own = prepare(pixel_factors, scene_factors, tiles[0])
    mine = other = None
    for step in range(STEPS):
        last = step + 1 == STEPS
        parts, whole = [], CALLS[step].index((0,))
        for n, chunks in enumerate(CALLS[step]):
            block = [mine[r] for r in chunks] + [other[r] for r in chunks] if step else blocks
            before = [parts[-1][1]] if parts else []
            if n == 2:
                carried, before = [parts[whole][0]], [*before, sums]
            else:
                carried = []
            parts.append(misfit_part(step, chunks, occupancy, factors, tiles, block, carried, before))
            if chunks == (2,):
                early = moved(parts[-1][0], core=1)
                sums = call(add_first_kernel, PIECE, [VMEM] * 2, VMEM, (parts[-1][1], early))
                arrived = [moved(sums, y=2)]
        if step:
            blocks = [p[4] for p in parts] + [p[5] for p in parts]
        late = moved(parts[2][0], core=1)
        sums = call(
            add_rest_kernel,
            [PIECE] * 3,
            [VMEM] * 3,
            [VMEM] * 3,
            (parts[2][1], parts[whole][1], late),
        )
        arrived += [moved(v, y=r) for r, v in zip((1, 3), sums)]
        half = call(total_kernel, PIECE, [VMEM] * 5, VMEM, (own, sums[2], *arrived))
        go = STEPS - 1 if last else -1
        far, near = moved(half, blk=go, zh=1), moved(half, blk=go)
        token, pixels, factors = pixel_step(step, pixels, parts, blocks, half)
        if not last:
            elevations, quality, token = lax.optimization_barrier((elevations, quality, token))
            tiles = elevations[step + 1], quality[step + 1]
        own = call(
            functools.partial(fresh_kernel, last),
            ROWS if last else PIECE,
            [VMEM] * 2 + [ANY],
            VMEM,
            (near, far, token),
        )
        mine, other = {0: own}, {}
        if not last:
            other[0] = moved(own, core=1)
        for r in ORDER:
            mine[r] = moved(own, y=-r)
        if not last:
            for r in ORDER:
                other[r] = moved(mine[r], core=1)
    joined = jax.ShapeDtypeStruct((N_Y, CHUNK, R), F32)
    joined = call(join_kernel, joined, [VMEM] * N_Y, VMEM, [mine[r] for r in range(N_Y)])
    scene = call(
        assemble_kernel,
        jax.ShapeDtypeStruct((ACQ_BLK, R), F32),
        [VMEM] * 2,
        HBM,
        (joined, moved(joined, core=1)),
        scratch=[pltpu.SemaphoreType.DMA((N_CORE, N_Y))],
    )
    return (pixels, scene)


def solution(mesh):
    in_specs = (
        P(("blk", "rep"), None),
        P("blk", None),
        P(None, ("blk", "rep"), None),
        P(None, ("blk", "rep"), None),
        P(None, ("blk", "rep")),
    )
    out_specs = (P(("blk", "rep"), None), P("blk", None))
    return jax.shard_map(steps, mesh=mesh, in_specs=in_specs, out_specs=out_specs, check_vma=False)
```

```python
import functools

import jax
import jax.numpy as jnp
from jax import lax
from jax.experimental import pallas as pl
from jax.experimental.pallas import tpu as pltpu
from jax.sharding import PartitionSpec as P


PIX_DEV = 768
ACQ_BLK = 1024
R = 256
STEPS = 3
GROUP_ROWS = 12288
N_BLK = 16
N_Y = 4
N_ZH = 2
N_CORE = 2
N_REP = N_Y * N_ZH * N_CORE
CHUNK = 128
PAIR = 2 * CHUNK
ROW_TILE = 256
BOTH = ("blk", "rep")
ORDER = (2, 1, 3)
CALLS = (((2,), (0,), (1, 3)), ((0,), (2,), (1, 3)), ((0,), (2,), (1, 3)))


VMEM = pl.BlockSpec(memory_space=pltpu.VMEM)
SMEM = pl.BlockSpec(memory_space=pltpu.SMEM)
HBM = pl.BlockSpec(memory_space=pltpu.HBM)
ANY = pl.BlockSpec(memory_space=pl.ANY)

F32, BF16 = jnp.float32, jnp.bfloat16
PIXELS = jax.ShapeDtypeStruct((PIX_DEV, R), F32)
HALF = jax.ShapeDtypeStruct((PIX_DEV, R), BF16)
TURNED = jax.ShapeDtypeStruct((R, PIX_DEV), BF16)
PIECE = jax.ShapeDtypeStruct((R, CHUNK), F32)
ROWS = jax.ShapeDtypeStruct((CHUNK, R), F32)
TOKEN = jax.ShapeDtypeStruct((8, 128), F32)
FLOPS = 3 * 2 * PIX_DEV * ACQ_BLK * R


def moved(value, blk=0, y=0, zh=0, core=0):
    pairs = []
    for b in range(N_BLK):
        for r in range(N_REP):
            ry, rz, rc = r // (N_ZH * N_CORE), (r // N_CORE) % N_ZH, r % N_CORE
            db = (b + blk) % N_BLK
            dr = (((ry + y) % N_Y) * N_ZH + (rz + zh) % N_ZH) * N_CORE + (rc + core) % N_CORE
            pairs.append((b * N_REP + r, db * N_REP + dr))
    return lax.ppermute(value, BOTH, pairs)


def position():
    rep = lax.axis_index("rep")
    return lax.rem(rep, N_CORE), lax.div(rep, N_ZH * N_CORE)


def split(value):
    high = value.astype(BF16)
    low = (value - high.astype(F32)).astype(BF16)
    return high, low


NN = (((1,), (0,)), ((), ()))
NT = (((1,), (1,)), ((), ()))


def dot3(a_high, a_low, b_high, b_low, dims):
    dot = functools.partial(lax.dot_general, dimension_numbers=dims, preferred_element_type=F32)
    return dot(a_high, b_high) + (dot(a_high, b_low) + dot(a_low, b_high))


def call(kernel, out, in_specs, out_specs, args, mib=4, flops=0, scratch=()):
    return pl.pallas_call(
        kernel,
        out_shape=out,
        in_specs=in_specs,
        out_specs=out_specs,
        scratch_shapes=list(scratch),
        compiler_params=pltpu.CompilerParams(vmem_limit_bytes=mib << 20),
        cost_estimate=pl.CostEstimate(flops=flops, bytes_accessed=1 << 20, transcendentals=0),
    )(*args)


def prepare_kernel(pixels, scene, before, uh, ul, uth, utl, vh, vl, own):
    core, y = position()

    @pl.loop(0, N_Y)
    def _(r):
        at = lax.rem(y + r, N_Y) * PAIR
        vh[r], vl[r] = split(scene[pl.ds(pl.multiple_of(at, PAIR), PAIR), :].T)

    own[...] = scene[pl.ds(pl.multiple_of(y * PAIR + core * CHUNK, CHUNK), CHUNK), :].T

    @pl.loop(0, PIX_DEV // ROW_TILE)
    def _(t):
        rows = pl.ds(pl.multiple_of(t * ROW_TILE, ROW_TILE), ROW_TILE)
        value = pixels[rows, :]
        uh[rows, :], ul[rows, :] = split(value)
        uth[:, rows], utl[:, rows] = split(value.T)


def prepare(pixels, scene, before):
    blocks = jax.ShapeDtypeStruct((N_Y, R, PAIR), BF16)
    out = [HALF, HALF, TURNED, TURNED, blocks, blocks, PIECE]
    res = call(prepare_kernel, out, [VMEM] * 2 + [ANY], [VMEM] * len(out), (pixels, scene, before))
    return res[:4], res[4:6], res[6]


def misfit_kernel(step, chunks, carried, occupancy, uh, ul, uth, utl, tile, weight, *refs):
    core, y = position()
    count = len(chunks)
    if step:
        mine, other, refs = refs[:count], refs[count : 2 * count], refs[2 * count :]
        refs, (vh, vl) = refs[:-2], refs[-2:]
        for k in range(count):
            first = jnp.where(core == 0, mine[k][...], other[k][...])
            second = jnp.where(core == 0, other[k][...], mine[k][...])
            vh[k], vl[k] = split(jnp.concatenate([first, second], axis=1))
    else:
        (vh, vl), refs = refs[:2], refs[2:]
    sent, kept, mh, ml = refs[-4:]
    if carried:
        sent[count] = refs[0][0]
    flag = occupancy[step, 0].astype(F32)

    def one(k, r, at):
        columns = pl.ds(pl.multiple_of(lax.rem(y + r, N_Y) * PAIR, PAIR), PAIR)
        v_high, v_low = vh[at], vl[at]
        predicted = dot3(uh[...], ul[...], v_high, v_low, NN)
        misfit = (weight[:, columns].astype(F32) * flag) * (tile[:, columns].astype(F32) - predicted)
        m_high, m_low = split(misfit)
        mh[k] = m_high
        ml[k] = m_low
        grad = dot3(uth[...], utl[...], m_high, m_low, NN)
        left, right = grad[:, :CHUNK], grad[:, CHUNK:]
        kept[k] = jnp.where(core == 0, left, right)
        sent[k] = jnp.where(core == 0, right, left)

    if count == 1:
        one(0, chunks[0], 0 if step else chunks[0])
    else:

        @pl.loop(0, count)
        def _(k):
            r = chunks[0] + k * (chunks[1] - chunks[0])
            one(k, r, k if step else r)


def misfit_part(step, chunks, occupancy, factors, tiles, block, carried, before):
    count = len(chunks)
    pieces = lambda n: jax.ShapeDtypeStruct((n, R, CHUNK), F32)
    misfits = jax.ShapeDtypeStruct((count, PIX_DEV, PAIR), BF16)
    blocks = jax.ShapeDtypeStruct((count, R, PAIR), BF16)
    out = [pieces(count + len(carried)), pieces(count), misfits, misfits] + ([blocks] * 2 if step else [])
    ins = [occupancy, *factors, *tiles, *block, *carried]
    return call(
        functools.partial(misfit_kernel, step, chunks, len(carried)),
        out,
        [SMEM] + [VMEM] * (len(ins) - 1) + [ANY] * len(before),
        [VMEM] * len(out),
        (*ins, *before),
        mib=6,
        flops=FLOPS * count // 2,
    )


def pixel_kernel(step, pixels, *refs):
    last = step + 1 == STEPS
    calls = len(CALLS[step])
    rows_of = [(n, k) for n, chunks in enumerate(CALLS[step]) for k in range(len(chunks))]
    mh, ml, refs = refs[:calls], refs[calls : 2 * calls], refs[2 * calls :]
    if step:
        vh, vl, refs = refs[:calls], refs[calls : 2 * calls], refs[2 * calls :]
    else:
        vh, vl, refs = refs[0], refs[1], refs[2:]
    outs = refs[1:]
    outs[0][...] = jnp.zeros_like(outs[0])

    @pl.loop(0, PIX_DEV // ROW_TILE)
    def _(t):
        rows = pl.ds(pl.multiple_of(t * ROW_TILE, ROW_TILE), ROW_TILE)
        grad = jnp.zeros((ROW_TILE, R), F32)
        for n, k in rows_of:
            r = CALLS[step][n][k]
            v_high, v_low = (vh[n][k], vl[n][k]) if step else (vh[r], vl[r])
            grad = grad + dot3(mh[n][k, rows, :], ml[n][k, rows, :], v_high, v_low, NT)
        value = pixels[rows, :] + (8.0 / ACQ_BLK) * grad
        outs[1][rows, :] = value
        if not last:
            outs[2][rows, :], outs[3][rows, :] = split(value)
            outs[4][:, rows], outs[5][:, rows] = split(value.T)


def pixel_step(step, pixels, parts, blocks, after):
    last = step + 1 == STEPS
    ins = [pixels, *(p[2] for p in parts), *(p[3] for p in parts), *blocks, after]
    out = [TOKEN, PIXELS]
    if not last:
        out += [HALF, HALF, TURNED, TURNED]
    res = call(
        functools.partial(pixel_kernel, step),
        out,
        [VMEM] * (len(ins) - 1) + [ANY],
        [VMEM] * len(out),
        ins,
        flops=FLOPS,
    )
    return res[0], res[1], res[2:]


def add_first_kernel(kept, swapped, out):
    out[...] = kept[0] + swapped[0]


def add_rest_kernel(kept, own, swapped, first, second, third):
    first[...] = kept[0] + swapped[0]
    second[...] = kept[1] + swapped[1]
    third[...] = own[0] + swapped[2]


def total_kernel(own, summed, first, second, third, out):
    total = summed[...] + (first[...] + (second[...] + third[...]))
    out[...] = 0.5 * own[...] + (8.0 / GROUP_ROWS) * total


def fresh_kernel(last, a, b, after, out):
    value = a[...] + b[...]
    out[...] = value.T if last else value


JOINED = (0,) + ORDER[:2]


def join_kernel(*refs):
    for k in range(len(JOINED)):
        refs[-1][k] = refs[k][...]


def assemble_kernel(mine, other, last_mine, last_other, out, sems):
    core, y = position()
    copies = []
    for k, (pieces, piece) in enumerate(((mine, last_mine), (other, last_other))):
        for n, r in enumerate(JOINED + ORDER[2:]):
            at = lax.rem(y + r, N_Y) * PAIR + lax.rem(core + k, N_CORE) * CHUNK
            rows = pl.ds(pl.multiple_of(at, CHUNK), CHUNK)
            source = pieces.at[n] if n < len(JOINED) else piece
            copies.append(pltpu.make_async_copy(source, out.at[rows, :], sems.at[k, n]))
    for c in copies:
        c.start()
    for c in copies:
        c.wait()


def steps(pixel_factors, scene_factors, elevations, quality, occupancy):
    pixels = pixel_factors
    tiles = elevations[0], quality[0]
    factors, blocks, own = prepare(pixel_factors, scene_factors, tiles[0])
    mine = other = None
    for step in range(STEPS):
        last = step + 1 == STEPS
        parts, whole = [], CALLS[step].index((0,))
        for n, chunks in enumerate(CALLS[step]):
            block = [mine[r] for r in chunks] + [other[r] for r in chunks] if step else blocks
            before = [parts[-1][1]] if parts else []
            if n == 2:
                carried, before = [parts[whole][0]], [*before, sums]
            else:
                carried = []
            parts.append(misfit_part(step, chunks, occupancy, factors, tiles, block, carried, before))
            if chunks == (2,):
                early = moved(parts[-1][0], core=1)
                sums = call(add_first_kernel, PIECE, [VMEM] * 2, VMEM, (parts[-1][1], early))
                arrived = [moved(sums, y=2)]
        if step:
            blocks = [p[4] for p in parts] + [p[5] for p in parts]
        late = moved(parts[2][0], core=1)
        sums = call(
            add_rest_kernel,
            [PIECE] * 3,
            [VMEM] * 3,
            [VMEM] * 3,
            (parts[2][1], parts[whole][1], late),
        )
        arrived += [moved(v, y=r) for r, v in zip((1, 3), sums)]
        half = call(total_kernel, PIECE, [VMEM] * 5, VMEM, (own, sums[2], *arrived))
        go = STEPS - 1 if last else -1
        far, near = moved(half, blk=go, zh=1), moved(half, blk=go)
        token, pixels, factors = pixel_step(step, pixels, parts, blocks, half)
        if not last:
            elevations, quality, token = lax.optimization_barrier((elevations, quality, token))
            tiles = elevations[step + 1], quality[step + 1]
        own = call(
            functools.partial(fresh_kernel, last),
            ROWS if last else PIECE,
            [VMEM] * 2 + [ANY],
            VMEM,
            (near, far, token),
        )
        mine, other = {0: own}, {}
        if not last:
            other[0] = moved(own, core=1)
        for r in ORDER:
            mine[r] = moved(own, y=-r)
        if not last:
            for r in ORDER:
                other[r] = moved(mine[r], core=1)
    joined = jax.ShapeDtypeStruct((len(JOINED), CHUNK, R), F32)
    joined = call(join_kernel, joined, [VMEM] * len(JOINED), VMEM, [mine[r] for r in JOINED])
    late = mine[ORDER[2]]
    scene = call(
        assemble_kernel,
        jax.ShapeDtypeStruct((ACQ_BLK, R), F32),
        [VMEM] * 4,
        HBM,
        (joined, moved(joined, core=1), late, moved(late, core=1)),
        scratch=[pltpu.SemaphoreType.DMA((N_CORE, N_Y))],
    )
    return (pixels, scene)


def solution(mesh):
    in_specs = (
        P(("blk", "rep"), None),
        P("blk", None),
        P(None, ("blk", "rep"), None),
        P(None, ("blk", "rep"), None),
        P(None, ("blk", "rep")),
    )
    out_specs = (P(("blk", "rep"), None), P("blk", None))
    return jax.shard_map(steps, mesh=mesh, in_specs=in_specs, out_specs=out_specs, check_vma=False)
```

```python
import functools

import jax
import jax.numpy as jnp
from jax import lax
from jax.experimental import pallas as pl
from jax.experimental.pallas import tpu as pltpu
from jax.sharding import PartitionSpec as P


PIX_DEV = 768
ACQ_BLK = 1024
R = 256
STEPS = 3
GROUP_ROWS = 12288
N_BLK = 16
N_Y = 4
N_ZH = 2
N_CORE = 2
N_REP = N_Y * N_ZH * N_CORE
CHUNK = 128
PAIR = 2 * CHUNK
ROW_TILE = 256
BOTH = ("blk", "rep")
ORDER = (2, 1, 3)
CALLS = (((2,), (0,), (1, 3)), ((0,), (2,), (1, 3)), ((0,), (2,), (1, 3)))


VMEM = pl.BlockSpec(memory_space=pltpu.VMEM)
SMEM = pl.BlockSpec(memory_space=pltpu.SMEM)
HBM = pl.BlockSpec(memory_space=pltpu.HBM)
ANY = pl.BlockSpec(memory_space=pl.ANY)

F32, BF16 = jnp.float32, jnp.bfloat16
PIXELS = jax.ShapeDtypeStruct((PIX_DEV, R), F32)
HALF = jax.ShapeDtypeStruct((PIX_DEV, R), BF16)
TURNED = jax.ShapeDtypeStruct((R, PIX_DEV), BF16)
PIECE = jax.ShapeDtypeStruct((R, CHUNK), F32)
ROWS = jax.ShapeDtypeStruct((CHUNK, R), F32)
TOKEN = jax.ShapeDtypeStruct((8, 128), F32)
FLOPS = 3 * 2 * PIX_DEV * ACQ_BLK * R


def moved(value, blk=0, y=0, zh=0, core=0):
    pairs = []
    for b in range(N_BLK):
        for r in range(N_REP):
            ry, rz, rc = r // (N_ZH * N_CORE), (r // N_CORE) % N_ZH, r % N_CORE
            db = (b + blk) % N_BLK
            dr = (((ry + y) % N_Y) * N_ZH + (rz + zh) % N_ZH) * N_CORE + (rc + core) % N_CORE
            pairs.append((b * N_REP + r, db * N_REP + dr))
    return lax.ppermute(value, BOTH, pairs)


def position():
    rep = lax.axis_index("rep")
    return lax.rem(rep, N_CORE), lax.div(rep, N_ZH * N_CORE)


def split(value):
    high = value.astype(BF16)
    low = (value - high.astype(F32)).astype(BF16)
    return high, low


NN = (((1,), (0,)), ((), ()))
NT = (((1,), (1,)), ((), ()))


def dot3(a_high, a_low, b_high, b_low, dims):
    dot = functools.partial(lax.dot_general, dimension_numbers=dims, preferred_element_type=F32)
    return dot(a_high, b_high) + (dot(a_high, b_low) + dot(a_low, b_high))


def call(kernel, out, in_specs, out_specs, args, mib=4, flops=0, scratch=()):
    return pl.pallas_call(
        kernel,
        out_shape=out,
        in_specs=in_specs,
        out_specs=out_specs,
        scratch_shapes=list(scratch),
        compiler_params=pltpu.CompilerParams(vmem_limit_bytes=mib << 20),
        cost_estimate=pl.CostEstimate(flops=flops, bytes_accessed=1 << 20, transcendentals=0),
    )(*args)


def prepare_kernel(pixels, scene, before, uh, ul, uth, utl, vh, vl, own):
    core, y = position()

    @pl.loop(0, N_Y)
    def _(r):
        at = lax.rem(y + r, N_Y) * PAIR
        vh[r], vl[r] = split(scene[pl.ds(pl.multiple_of(at, PAIR), PAIR), :].T)

    own[...] = scene[pl.ds(pl.multiple_of(y * PAIR + core * CHUNK, CHUNK), CHUNK), :].T

    @pl.loop(0, PIX_DEV // ROW_TILE)
    def _(t):
        rows = pl.ds(pl.multiple_of(t * ROW_TILE, ROW_TILE), ROW_TILE)
        value = pixels[rows, :]
        uh[rows, :], ul[rows, :] = split(value)
        uth[:, rows], utl[:, rows] = split(value.T)


def prepare(pixels, scene, before):
    blocks = jax.ShapeDtypeStruct((N_Y, R, PAIR), BF16)
    out = [HALF, HALF, TURNED, TURNED, blocks, blocks, PIECE]
    res = call(prepare_kernel, out, [VMEM] * 2 + [ANY], [VMEM] * len(out), (pixels, scene, before))
    return res[:4], res[4:6], res[6]


def misfit_kernel(step, chunks, carried, occupancy, uh, ul, uth, utl, tile, weight, *refs):
    core, y = position()
    count = len(chunks)
    if step:
        mine, other, refs = refs[:count], refs[count : 2 * count], refs[2 * count :]
        refs, (vh, vl) = refs[:-2], refs[-2:]
        for k in range(count):
            first = jnp.where(core == 0, mine[k][...], other[k][...])
            second = jnp.where(core == 0, other[k][...], mine[k][...])
            vh[k], vl[k] = split(jnp.concatenate([first, second], axis=1))
    else:
        (vh, vl), refs = refs[:2], refs[2:]
    sent, kept, mh, ml = refs[-4:]
    if carried:
        sent[count] = refs[0][0]
    flag = occupancy[0, step].astype(F32)

    def one(k, r, at):
        columns = pl.ds(pl.multiple_of(lax.rem(y + r, N_Y) * PAIR, PAIR), PAIR)
        v_high, v_low = vh[at], vl[at]
        predicted = dot3(uh[...], ul[...], v_high, v_low, NN)
        misfit = (weight[:, columns].astype(F32) * flag) * (tile[:, columns].astype(F32) - predicted)
        m_high, m_low = split(misfit)
        mh[k] = m_high
        ml[k] = m_low
        grad = dot3(uth[...], utl[...], m_high, m_low, NN)
        left, right = grad[:, :CHUNK], grad[:, CHUNK:]
        kept[k] = jnp.where(core == 0, left, right)
        sent[k] = jnp.where(core == 0, right, left)

    if count == 1:
        one(0, chunks[0], 0 if step else chunks[0])
    else:

        @pl.loop(0, count)
        def _(k):
            r = chunks[0] + k * (chunks[1] - chunks[0])
            one(k, r, k if step else r)


def misfit_part(step, chunks, occupancy, factors, tiles, block, carried, before):
    count = len(chunks)
    pieces = lambda n: jax.ShapeDtypeStruct((n, R, CHUNK), F32)
    misfits = jax.ShapeDtypeStruct((count, PIX_DEV, PAIR), BF16)
    blocks = jax.ShapeDtypeStruct((count, R, PAIR), BF16)
    out = [pieces(count + len(carried)), pieces(count), misfits, misfits] + ([blocks] * 2 if step else [])
    ins = [occupancy, *factors, *tiles, *block, *carried]
    return call(
        functools.partial(misfit_kernel, step, chunks, len(carried)),
        out,
        [SMEM] + [VMEM] * (len(ins) - 1) + [ANY] * len(before),
        [VMEM] * len(out),
        (*ins, *before),
        mib=6,
        flops=FLOPS * count // 2,
    )


def pixel_kernel(step, pixels, *refs):
    last = step + 1 == STEPS
    calls = len(CALLS[step])
    rows_of = [(n, k) for n, chunks in enumerate(CALLS[step]) for k in range(len(chunks))]
    mh, ml, refs = refs[:calls], refs[calls : 2 * calls], refs[2 * calls :]
    if step:
        vh, vl, refs = refs[:calls], refs[calls : 2 * calls], refs[2 * calls :]
    else:
        vh, vl, refs = refs[0], refs[1], refs[2:]
    outs = refs[1:]
    outs[0][...] = jnp.zeros_like(outs[0])

    @pl.loop(0, PIX_DEV // ROW_TILE)
    def _(t):
        rows = pl.ds(pl.multiple_of(t * ROW_TILE, ROW_TILE), ROW_TILE)
        grad = jnp.zeros((ROW_TILE, R), F32)
        for n, k in rows_of:
            r = CALLS[step][n][k]
            v_high, v_low = (vh[n][k], vl[n][k]) if step else (vh[r], vl[r])
            grad = grad + dot3(mh[n][k, rows, :], ml[n][k, rows, :], v_high, v_low, NT)
        value = pixels[rows, :] + (8.0 / ACQ_BLK) * grad
        outs[1][rows, :] = value
        if not last:
            outs[2][rows, :], outs[3][rows, :] = split(value)
            outs[4][:, rows], outs[5][:, rows] = split(value.T)


def pixel_step(step, pixels, parts, blocks, after):
    last = step + 1 == STEPS
    ins = [pixels, *(p[2] for p in parts), *(p[3] for p in parts), *blocks, after]
    out = [TOKEN, PIXELS]
    if not last:
        out += [HALF, HALF, TURNED, TURNED]
    res = call(
        functools.partial(pixel_kernel, step),
        out,
        [VMEM] * (len(ins) - 1) + [ANY],
        [VMEM] * len(out),
        ins,
        flops=FLOPS,
    )
    return res[0], res[1], res[2:]


def add_first_kernel(kept, swapped, out):
    out[...] = kept[0] + swapped[0]


def add_rest_kernel(kept, own, swapped, first, second, third):
    first[...] = kept[0] + swapped[0]
    second[...] = kept[1] + swapped[1]
    third[...] = own[0] + swapped[2]


def total_kernel(own, summed, first, second, third, out):
    total = summed[...] + (first[...] + (second[...] + third[...]))
    out[...] = 0.5 * own[...] + (8.0 / GROUP_ROWS) * total


def fresh_kernel(last, a, b, after, out):
    value = a[...] + b[...]
    out[...] = value.T if last else value


JOINED = (0,) + ORDER[:2]


def join_kernel(*refs):
    for k in range(len(JOINED)):
        refs[-1][k] = refs[k][...]


def assemble_kernel(mine, other, last_mine, last_other, out, sems):
    core, y = position()
    copies = []
    for k, (pieces, piece) in enumerate(((mine, last_mine), (other, last_other))):
        for n, r in enumerate(JOINED + ORDER[2:]):
            at = lax.rem(y + r, N_Y) * PAIR + lax.rem(core + k, N_CORE) * CHUNK
            rows = pl.ds(pl.multiple_of(at, CHUNK), CHUNK)
            source = pieces.at[n] if n < len(JOINED) else piece
            copies.append(pltpu.make_async_copy(source, out.at[rows, :], sems.at[k, n]))
    for c in copies:
        c.start()
    for c in copies:
        c.wait()


def per_device(pixel_factors, scene_factors, elevations, quality, occupancy):
    return steps(pixel_factors, scene_factors, elevations, quality, occupancy.T)


def steps(pixel_factors, scene_factors, elevations, quality, occupancy):
    pixels = pixel_factors
    tiles = elevations[0], quality[0]
    factors, blocks, own = prepare(pixel_factors, scene_factors, tiles[0])
    mine = other = None
    for step in range(STEPS):
        last = step + 1 == STEPS
        parts, whole = [], CALLS[step].index((0,))
        for n, chunks in enumerate(CALLS[step]):
            block = [mine[r] for r in chunks] + [other[r] for r in chunks] if step else blocks
            before = [parts[-1][1]] if parts else []
            if n == 2:
                carried, before = [parts[whole][0]], [*before, sums]
            else:
                carried = []
            parts.append(misfit_part(step, chunks, occupancy, factors, tiles, block, carried, before))
            if chunks == (2,):
                early = moved(parts[-1][0], core=1)
                sums = call(add_first_kernel, PIECE, [VMEM] * 2, VMEM, (parts[-1][1], early))
                arrived = [moved(sums, y=2)]
        if step:
            blocks = [p[4] for p in parts] + [p[5] for p in parts]
        late = moved(parts[2][0], core=1)
        sums = call(
            add_rest_kernel,
            [PIECE] * 3,
            [VMEM] * 3,
            [VMEM] * 3,
            (parts[2][1], parts[whole][1], late),
        )
        arrived += [moved(v, y=r) for r, v in zip((1, 3), sums)]
        half = call(total_kernel, PIECE, [VMEM] * 5, VMEM, (own, sums[2], *arrived))
        go = STEPS - 1 if last else -1
        far, near = moved(half, blk=go, zh=1), moved(half, blk=go)
        token, pixels, factors = pixel_step(step, pixels, parts, blocks, half)
        if not last:
            elevations, quality, token = lax.optimization_barrier((elevations, quality, token))
            tiles = elevations[step + 1], quality[step + 1]
        own = call(
            functools.partial(fresh_kernel, last),
            ROWS if last else PIECE,
            [VMEM] * 2 + [ANY],
            VMEM,
            (near, far, token),
        )
        mine, other = {0: own}, {}
        if not last:
            other[0] = moved(own, core=1)
        for r in ORDER:
            mine[r] = moved(own, y=-r)
        if not last:
            for r in ORDER:
                other[r] = moved(mine[r], core=1)
    joined = jax.ShapeDtypeStruct((len(JOINED), CHUNK, R), F32)
    joined = call(join_kernel, joined, [VMEM] * len(JOINED), VMEM, [mine[r] for r in JOINED])
    late = mine[ORDER[2]]
    scene = call(
        assemble_kernel,
        jax.ShapeDtypeStruct((ACQ_BLK, R), F32),
        [VMEM] * 4,
        HBM,
        (joined, moved(joined, core=1), late, moved(late, core=1)),
        scratch=[pltpu.SemaphoreType.DMA((N_CORE, N_Y))],
    )
    return (pixels, scene)


def solution(mesh):
    in_specs = (
        P(("blk", "rep"), None),
        P("blk", None),
        P(None, ("blk", "rep"), None),
        P(None, ("blk", "rep"), None),
        P(None, ("blk", "rep")),
    )
    out_specs = (P(("blk", "rep"), None), P("blk", None))
    return jax.shard_map(
        per_device, mesh=mesh, in_specs=in_specs, out_specs=out_specs, check_vma=False
    )
```
